32 devices in a mesh: pb: 8 (over z, core), tile: 4 (over y, x).
Axes of the slice: x: 2, y: 2, z: 4, core: 2. Of those that a mesh axis runs over, the one named last changes fastest.
Arguments:
- trials: bfloat16 [16, 4, 4096], P('pb', None, 'tile'), may hold values from -6 to 6
- w_screen: bfloat16 [16, 2048, 2048], P('pb', 'tile'), may hold values from -48 to 48
- cond_bands: bfloat16 [16, 2048, 64], P('pb', 'tile'), may hold values from -0.125 to 0.125
- val_bands: bfloat16 [16, 2048, 64], P('pb', 'tile'), may hold values from -0.125 to 0.125
- pair_table: int32 [16, 16], replicated, may hold values from 0 to 15, as said below
Outputs:
- applied: bfloat16 [16, 4, 4096], P('pb', None, 'tile')
The draws below stay inside these ranges and needn't reach their ends.
Inputs may be any that keep to these rules, and one draw needn't show every extreme that they name: Every row and every column of pair_table holds each k-point exactly once.
All inputs are finite; a program needn't handle non-finite values.
Results may differ from the reference program's by a relative error of at most 0.023.
Values may be sent and summed in bfloat16 or wider, within the bound.
No kernel may reach another device: no remote copies, remote signals or barrier semaphores. Data moves between devices by JAX's collectives and lax.ppermute only.
A program may use at most 128 MiB of HBM per device.

```python
import jax
import jax.numpy as jnp
from jax import lax

NK = 16
NS = 4
NP = 2048
NC = 64
NV = 64


def draw_pair_table(key, part):
    labels = jax.random.permutation(jax.random.fold_in(key, 7), NK)
    places = jnp.argsort(labels)
    differ = (places[:, None] - places[None, :]) % NK
    return labels[differ].astype(jnp.int32)


def levels(rng, extent, pieces, least, largest):
    gain, own = 1.0, jax.random.fold_in(rng, 6)
    for axis_at, blocks in pieces:
        draws = jnp.exp(jax.random.uniform(jax.random.fold_in(own, axis_at), (blocks,), jnp.float32, least / len(pieces), largest / len(pieces)))
        gain = gain * jnp.repeat(draws, extent[axis_at] // blocks).reshape([-1 if axis == axis_at else 1 for axis in range(len(extent))])
    return gain


def bell_draw(key, dims, deviation, limit, split=(), kind=jnp.bfloat16):
    level = levels(key, dims, split, -0.22, 0.18) if split else 1.0
    entries = jax.random.normal(key, dims, jnp.float32) * deviation * level
    return jnp.minimum(jnp.maximum(entries, -limit), limit).astype(kind)


def setup_inputs(seed: int = 0) -> dict:
    streams_of = jax.random.split(jax.random.key(seed), 6)
    return {
        "trials": bell_draw(streams_of[0], (NK, NS, NC * NV), 1.0, 6.0, ((0, 8), (2, 4))),
        "w_screen": bell_draw(streams_of[1], (NK, NP, NP), 8.0, 48.0, ((0, 8), (1, 4))),
        "cond_bands": bell_draw(streams_of[2], (NK, NP, NC), NP ** -0.5, 0.125, ((0, 8), (1, 4))),
        "val_bands": bell_draw(streams_of[3], (NK, NP, NV), NP ** -0.5, 0.125, ((0, 8), (1, 4))),
        "pair_table": draw_pair_table(jax.random.fold_in(streams_of[5], 71), 0),
    }


def reference(trials, w_screen, cond_bands, val_bands, pair_table):
    xmat = trials.reshape(NK, NS, NC, NV).astype(jnp.float32)
    cond_all = cond_bands.astype(jnp.float32)
    val_all = val_bands.astype(jnp.float32)
    amat = jnp.einsum('kpc,kscv->kspv', cond_all, xmat).astype(jnp.bfloat16)

    def one_pair(carry, index):
        qpoint = index // NK
        kpoint = index % NK
        kprime = pair_table[kpoint, qpoint]
        mmat = jnp.einsum('spv,nv->spn', amat[kprime].astype(jnp.float32), val_all[kprime])
        pmat = (mmat * w_screen[qpoint].astype(jnp.float32)).astype(jnp.bfloat16).astype(jnp.float32)
        gmat = jnp.einsum('pc,spn->scn', cond_all[kpoint], pmat).astype(jnp.bfloat16).astype(jnp.float32)
        contrib = jnp.einsum('scn,nv->scv', gmat, val_all[kpoint])
        return carry.at[kpoint].add(contrib), None

    start = jnp.zeros((NK, NS, NC, NV), jnp.float32)
    total, unused = lax.scan(one_pair, start, jnp.arange(NK * NK, dtype=jnp.int32))
    return total.reshape(NK, NS, NC * NV).astype(jnp.bfloat16)
```

```python
import functools

import jax
import jax.numpy as jnp
from jax import lax
from jax.experimental import pallas as pl
from jax.experimental.pallas import tpu as pltpu
from jax.sharding import PartitionSpec as P

F32, BF16 = jnp.float32, jnp.bfloat16


def tree_sum(terms):
    while len(terms) > 1:
        half = [terms[i] + terms[i + 1] for i in range(0, len(terms) - 1, 2)]
        terms = half + terms[len(half) * 2 :]
    return terms[0]


def stage_kernel(kc, nv, rows, pairs, place, uct_ref, x_ref, uvt_ref, wa_ref, wb_ref, yin_ref, y_ref, m_ref):
    nk, ns, npts, nblk = m_ref.shape
    qper = wa_ref.shape[0]
    here = place[0]

    def first(k, carry):
        a = lax.dot_general(
            uct_ref[k], x_ref[k], (((0,), (0,)), ((), ())), preferred_element_type=F32
        ).astype(BF16)
        uvt = uvt_ref[k]
        zero = jnp.zeros_like(uvt)
        for s in range(ns):
            rhs = jnp.concatenate([uvt if i == s else zero for i in range(ns)], axis=0)
            m_ref[k, s] = jnp.dot(a, rhs, preferred_element_type=F32).astype(BF16)
        return carry

    lax.fori_loop(0, nk, first, 0)

    def second(k, carry):
        kreal = ((k // kc) ^ here) * kc + k % kc
        idx = []
        for side in range(2):
            for q in range(qper):
                found = pairs[kreal, (here ^ side) * qper + q]
                idx.append(((found // kc) ^ here) * kc + found % kc)
        uv = uvt_ref[k].T
        zero = jnp.zeros_like(uv)
        rhs = jnp.concatenate(
            [jnp.concatenate([uv if i == s else zero for i in range(ns)], axis=1) for s in range(ns)], axis=0
        )
        parts = []
        for p in range(0, npts, rows):
            wq = [w[q, p : p + rows, :] for w in (wa_ref, wb_ref) for q in range(qper)]
            summed = [
                tree_sum([w * m_ref[i, s, p : p + rows, :] for w, i in zip(wq, idx)]) for s in range(ns)
            ]
            parts.append(
                jnp.dot(jnp.concatenate(summed, axis=1), rhs, preferred_element_type=F32).astype(BF16)
            )
        h = jnp.concatenate(parts, axis=0)
        y_ref[k] = yin_ref[k] + jnp.dot(uct_ref[k], h, preferred_element_type=F32)
        return carry

    lax.fori_loop(0, nk, second, 0)


def stage(step, kc, pairs, place, uct, x, uvt, wa, wb, y):
    nk, nc, npts = uct.shape
    nv, nblk = uvt.shape[1:]
    ns = x.shape[2] // nv
    nq = wa.shape[0] + wb.shape[0]

    def full(a):
        return pl.BlockSpec(a.shape, lambda i, pr, at: (0,) * a.ndim)

    return pl.pallas_call(
        functools.partial(stage_kernel, kc, nv, min(128, npts)),
        grid_spec=pltpu.PrefetchScalarGridSpec(
            num_scalar_prefetch=2,
            grid=(1,),
            in_specs=[
                full(uct),
                full(x),
                full(uvt),
                pl.BlockSpec(
                    (wa.shape[0], npts, nblk), lambda i, pr, at: (0, 0, (at[1] ^ step) * 2 + at[0] % 2)
                ),
                pl.BlockSpec((wb.shape[0], npts, nblk), lambda i, pr, at: (0, 0, at[1] ^ step)),
                full(y),
            ],
            out_specs=full(y),
            scratch_shapes=[pltpu.VMEM((nk, ns, npts, nblk), BF16)],
        ),
        out_shape=jax.ShapeDtypeStruct(y.shape, F32),
        input_output_aliases={7: 0},
        cost_estimate=pl.CostEstimate(
            flops=16 * nk * ns * npts * nblk * nv, bytes_accessed=8 * nq * npts * nblk, transcendentals=0
        ),
        compiler_params=pltpu.CompilerParams(
            vmem_limit_bytes=40 << 20, dimension_semantics=("arbitrary",)
        ),
    )(pairs, place, uct, x, uvt, wa, wb, y)


def shards(npb, ntile, trials, w_screen, cond_bands, val_bands, pair_table):
    kc, ns, _ = trials.shape
    qc, npts, ncols = w_screen.shape
    nc, nv = cond_bands.shape[2], val_bands.shape[2]
    width = val_bands.shape[1]
    half = width // 2
    nk = kc * npb
    cblk = nc // ntile
    here, tile = lax.axis_index("pb"), lax.axis_index("tile")
    core = here % 2

    def swap(a, axis, d):
        n = npb if axis == "pb" else ntile
        return lax.ppermute(a, axis, [(i, i ^ d) for i in range(n)])

    place = jnp.where(jnp.arange(2) == 0, here, tile).astype(jnp.int32)

    xt = trials.reshape(kc, ns, cblk, nv).transpose(0, 2, 1, 3).reshape(kc, cblk, ns * nv)
    xts = [xt] + [swap(xt, "tile", d) for d in range(1, ntile)]
    uvh = val_bands.transpose(0, 2, 1)
    lower, upper = uvh[:, :, :half], uvh[:, :, half:]
    uv_got = swap(jnp.where(core == 0, upper, lower), "pb", 1)
    uv_own = jnp.where(core == 0, lower, upper)

    x_own = jnp.stack(xts)[jnp.arange(ntile) ^ tile].transpose(1, 0, 2, 3).reshape(kc, nc, ns * nv)
    packed = jnp.concatenate([cond_bands.transpose(0, 2, 1), x_own, uv_own, uv_got], axis=2)
    packs = jnp.stack([packed] + [swap(packed, "pb", d) for d in range(2, npb, 2)])
    cut = npts + ns * nv
    even = packs[..., :cut]
    odd = swap(even, "pb", 1)

    w_sent = jnp.concatenate(
        [
            lax.dynamic_slice_in_dim(w_screen, i * width + (1 - core) * half, half, 2)
            for i in range(ntile)
        ],
        axis=2,
    )
    w_got = swap(w_sent, "pb", 1)

    both = jnp.stack([even, odd], axis=1).reshape(nk, nc, cut)
    uct, x = both[..., :npts], both[..., npts:]
    uvt = jnp.stack([packs[..., cut : cut + half], packs[..., cut + half :]], axis=1).reshape(nk, nv, half)

    y = jnp.zeros((nk, nc, ns * nv), F32)
    uvts = [uvt] + [swap(uvt, "tile", d) for d in range(1, ntile)]
    for d in range(ntile):
        y = stage(d, kc, pair_table, place, uct, x, uvts[d], w_screen, w_got, y)

    y = y.reshape(npb // 2, 2, kc, nc, ns * nv)
    y = y[:, 0] + swap(y[:, 1].astype(BF16), "pb", 1).astype(F32)
    y = y.reshape(npb // 2, kc, ntile, cblk, ns * nv)

    def block(d):
        return lax.dynamic_index_in_dim(y, tile ^ d, 2, keepdims=False)

    y = sum(
        [swap(block(d).astype(BF16), "tile", d).astype(F32) for d in range(1, ntile)], start=block(0)
    )
    y = sum(
        [swap(y[d].astype(BF16), "pb", 2 * d).astype(F32) for d in range(1, npb // 2)], start=y[0]
    )
    out = y.reshape(kc, cblk, ns, nv).transpose(0, 2, 1, 3)
    return out.reshape(kc, ns, cblk * nv).astype(BF16)


def solution(mesh):
    in_specs = (
        P("pb", None, "tile"),
        P("pb", "tile", None),
        P("pb", "tile", None),
        P("pb", "tile", None),
        P(),
    )
    out_specs = P("pb", None, "tile")
    body = functools.partial(shards, mesh.shape["pb"], mesh.shape["tile"])
    return jax.shard_map(body, mesh=mesh, in_specs=in_specs, out_specs=out_specs, check_vma=False)
```

```python
import functools

import jax
import jax.numpy as jnp
from jax import lax
from jax.experimental import pallas as pl
from jax.experimental.pallas import tpu as pltpu
from jax.sharding import PartitionSpec as P

F32, BF16 = jnp.float32, jnp.bfloat16
ROWS, U0, U1, U3 = 16, 4, 4, 4


def tree_sum(terms):
    while len(terms) > 1:
        half = [terms[i] + terms[i + 1] for i in range(0, len(terms) - 1, 2)]
        terms = half + terms[len(half) * 2 :]
    return terms[0]


def looped(n, unroll, step):
    unroll = unroll if n % unroll == 0 else 1

    def several(i, carry):
        for j in range(unroll):
            step(i * unroll + j)
        return carry

    lax.fori_loop(0, n // unroll, several, 0)


def stage_kernel(kc, nv, rows, pairs, place, uct_ref, x_ref, uvt_ref, *rest):
    *w_refs, yin_ref, y_ref, m_ref, a_ref, e_ref, h_ref, s0_ref, s1_ref = rest
    slots = (s0_ref, s1_ref)
    nk, ns, npts, nblk = m_ref.shape
    qper = w_refs[0].shape[0]
    here = place[0]

    def prepare(k):
        a_ref[k] = lax.dot_general(
            uct_ref[k], x_ref[k], (((0,), (0,)), ((), ())), preferred_element_type=F32
        ).astype(BF16)
        uv = uvt_ref[k].T
        zero = jnp.zeros_like(uv)
        for s in range(ns):
            e_ref[k, s * nblk : (s + 1) * nblk, :] = jnp.concatenate(
                [uv if i == s else zero for i in range(ns)], axis=1
            )

    looped(nk, U0, prepare)

    def mmats(k):
        uvt = uvt_ref[k]
        zero = jnp.zeros_like(uvt)
        for s in range(ns):
            rhs = jnp.concatenate([uvt if i == s else zero for i in range(ns)], axis=0)
            m_ref[k, s] = jnp.dot(a_ref[k], rhs, preferred_element_type=F32).astype(BF16)

    looped(nk, U1, mmats)

    def build(k, slot):
        kreal = ((k // kc) ^ here) * kc + k % kc
        idx = []
        for side in range(len(w_refs)):
            for q in range(qper):
                found = pairs[kreal, (here ^ side) * qper + q]
                idx.append(((found // kc) ^ here) * kc + found % kc)
        for p in range(0, npts, rows):
            wq = [w[q, p : p + rows, :] for w in w_refs for q in range(qper)]
            for s in range(ns):
                slot[p : p + rows, s * nblk : (s + 1) * nblk] = tree_sum(
                    [w * m_ref[i, s, p : p + rows, :] for w, i in zip(wq, idx)]
                )

    def contract(k, slot):
        h_ref[k] = jnp.dot(slot[...], e_ref[k], preferred_element_type=F32).astype(BF16)

    build(0, slots[0])

    def second(i, carry):
        for j in range(2):
            k = 2 * i + j
            contract(k, slots[j])
            build(jnp.minimum(k + 1, nk - 1), slots[1 - j])
        return carry

    lax.fori_loop(0, nk // 2, second, 0)

    def project(k):
        y_ref[k] = yin_ref[k] + jnp.dot(uct_ref[k], h_ref[k], preferred_element_type=F32)

    looped(nk, U3, project)


def stage(step, at_chunk, kc, pairs, place, uct, x, uvt, w_own, w_near, w_far, y):
    nk, nc, npts = uct.shape
    nv, nblk = uvt.shape[1:]
    ns = x.shape[2] // nv
    qper = w_own.shape[0]

    def full(a):
        return pl.BlockSpec(a.shape, lambda i, pr, at: (0,) * a.ndim)

    own_spec = pl.BlockSpec(
        (qper, npts, nblk),
        lambda i, pr, at: (0, (at[0] // 2) % 2, (at[1] ^ step) * 2 + at[0] % 2),
    )
    near_spec = pl.BlockSpec((qper, npts, nblk), lambda i, pr, at: (0, 0, step))
    far_spec = pl.BlockSpec((qper, npts, nblk), lambda i, pr, at: (0, 0, at_chunk))
    return pl.pallas_call(
        functools.partial(stage_kernel, kc, nv, ROWS),
        grid_spec=pltpu.PrefetchScalarGridSpec(
            num_scalar_prefetch=2,
            grid=(1,),
            in_specs=[full(uct), full(x), full(uvt), own_spec, near_spec, far_spec, far_spec, full(y)],
            out_specs=full(y),
            scratch_shapes=[
                pltpu.VMEM((nk, ns, npts, nblk), BF16),
                pltpu.VMEM((nk, npts, ns * nv), BF16),
                pltpu.VMEM((nk, ns * nblk, ns * nv), BF16),
                pltpu.VMEM((nk, npts, ns * nv), BF16),
                pltpu.VMEM((npts, ns * nblk), BF16),
                pltpu.VMEM((npts, ns * nblk), BF16),
            ],
        ),
        out_shape=jax.ShapeDtypeStruct(y.shape, F32),
        input_output_aliases={9: 0},
        cost_estimate=pl.CostEstimate(
            flops=16 * nk * ns * npts * nblk * nv, bytes_accessed=32 * qper * npts * nblk, transcendentals=0
        ),
        compiler_params=pltpu.CompilerParams(
            vmem_limit_bytes=40 << 20, dimension_semantics=("arbitrary",)
        ),
    )(pairs, place, uct, x, uvt, w_own, w_near, *w_far, y)


def shards(npb, ntile, trials, w_screen, cond_bands, val_bands, pair_table):
    kc, ns, _ = trials.shape
    qc, npts, ncols = w_screen.shape
    nc, nv = cond_bands.shape[2], val_bands.shape[2]
    width = val_bands.shape[1]
    half = width // 2
    nk = kc * npb
    cblk = nc // ntile
    here, tile = lax.axis_index("pb"), lax.axis_index("tile")
    core, part = here % 2, (here // 2) % 2
    prow = npts // 2

    def swap(a, axis, d):
        n = npb if axis == "pb" else ntile
        return lax.ppermute(a, axis, [(i, i ^ d) for i in range(n)])

    place = jnp.where(jnp.arange(2) == 0, here, tile).astype(jnp.int32)

    uvh = val_bands.transpose(0, 2, 1)
    lower, upper = uvh[:, :, :half], uvh[:, :, half:]
    uv_got = swap(jnp.where(core == 0, upper, lower), "pb", 1)
    uv_own = jnp.where(core == 0, lower, upper)
    xt = trials.reshape(kc, ns, cblk, nv).transpose(0, 2, 1, 3).reshape(kc, cblk, ns * nv)
    xts = [xt] + [swap(xt, "tile", d) for d in range(1, ntile)]

    ucth = cond_bands.transpose(0, 2, 1)
    first, second = ucth[:, :, :prow], ucth[:, :, prow:]
    uct_mine, uct_other = jnp.where(part == 0, first, second), jnp.where(part == 0, second, first)
    packed = [jnp.concatenate([u, uv_own, uv_got], axis=2) for u in (uct_mine, uct_other)]
    packs = jnp.stack([packed[0]] + [swap(packed[(d // 2) % 2], "pb", d) for d in range(2, npb, 2)])
    x_own = jnp.stack(xts)[jnp.arange(ntile) ^ tile].transpose(1, 0, 2, 3).reshape(kc, nc, ns * nv)
    x_even = jnp.stack([x_own] + [swap(x_own, "pb", d) for d in range(2, npb, 2)])
    even = jnp.concatenate([packs[..., :prow], x_even], axis=3)
    odd = swap(even, "pb", 1)
    both = jnp.stack([even, odd], axis=1).reshape(nk, nc, prow + ns * nv)
    uct, x = both[..., :prow], both[..., prow:]
    uvt = jnp.stack([packs[..., prow : prow + half], packs[..., prow + half :]], axis=1)
    uvt = uvt.reshape(nk, nv, half)
    uvts = [uvt] + [swap(uvt, "tile", d) for d in range(1, ntile)]

    def w_part(side, steps, after):
        rows = lax.dynamic_slice_in_dim(w_screen, (part ^ (side // 2)) * prow, prow, 1)
        cut = jnp.concatenate(
            [
                lax.dynamic_slice_in_dim(rows, (tile ^ i) * width + (core ^ (side % 2)) * half, half, 2)
                for i in steps
            ],
            axis=2,
        )
        if after is not None:
            cut, _ = lax.optimization_barrier((cut, after))
        return swap(cut, "pb", side)

    chunks = [range(1), range(1, 2), range(2, ntile)]
    near = w_part(1, range(ntile), None)
    y = jnp.zeros((nk, nc, ns * nv), F32)
    far = [[w_part(side, chunks[0], None) for side in (2, 3)]]
    far.append([w_part(side, chunks[1], packs) for side in (2, 3)])
    for d in range(ntile):
        c = min(d, 2)
        if d == 1:
            far.append([w_part(side, chunks[2], y) for side in (2, 3)])
        y = stage(d, d - chunks[c][0], kc, pair_table, place, uct, x, uvts[d], w_screen, near, far[c], y)

    y = y.reshape(npb // 2, 2, kc, nc, ns * nv)
    y = y[:, 0] + swap(y[:, 1].astype(BF16), "pb", 1).astype(F32)
    y = y.reshape(npb // 2, kc, ntile, cblk, ns * nv)

    def block(d):
        return lax.dynamic_index_in_dim(y, tile ^ d, 2, keepdims=False)

    y = sum(
        [swap(block(d).astype(BF16), "tile", d).astype(F32) for d in range(1, ntile)], start=block(0)
    )
    y = sum(
        [swap(y[d].astype(BF16), "pb", 2 * d).astype(F32) for d in range(1, npb // 2)], start=y[0]
    )
    out = y.reshape(kc, cblk, ns, nv).transpose(0, 2, 1, 3)
    return out.reshape(kc, ns, cblk * nv).astype(BF16)


def solution(mesh):
    in_specs = (
        P("pb", None, "tile"),
        P("pb", "tile", None),
        P("pb", "tile", None),
        P("pb", "tile", None),
        P(),
    )
    out_specs = P("pb", None, "tile")
    body = functools.partial(shards, mesh.shape["pb"], mesh.shape["tile"])
    return jax.shard_map(body, mesh=mesh, in_specs=in_specs, out_specs=out_specs, check_vma=False)
```

```python
import functools

import jax
import jax.numpy as jnp
from jax import lax
from jax.experimental import pallas as pl
from jax.experimental.pallas import tpu as pltpu
from jax.sharding import PartitionSpec as P

F32, BF16 = jnp.float32, jnp.bfloat16
ROWS, U0, U1, U3 = 16, 4, 4, 4


def tree_sum(terms):
    while len(terms) > 1:
        half = [terms[i] + terms[i + 1] for i in range(0, len(terms) - 1, 2)]
        terms = half + terms[len(half) * 2 :]
    return terms[0]


def looped(n, unroll, step):
    unroll = unroll if n % unroll == 0 else 1

    def several(i, carry):
        for j in range(unroll):
            step(i * unroll + j)
        return carry

    lax.fori_loop(0, n // unroll, several, 0)


def stage_kernel(kc, rows, pairs, place, uct_ref, x_ref, uvt_ref, *rest):
    *w_refs, yin_ref, y_ref, m_ref, a_ref, e_ref, h_ref, s0_ref, s1_ref = rest
    slots = (s0_ref, s1_ref)
    nk, ns, npts, nblk = m_ref.shape
    qper = w_refs[0].shape[0]
    here = place[0]

    def prepare(k):
        a_ref[k] = lax.dot_general(
            uct_ref[k], x_ref[k], (((0,), (0,)), ((), ())), preferred_element_type=F32
        ).astype(BF16)
        uv = uvt_ref[k].T
        zero = jnp.zeros_like(uv)
        for s in range(ns):
            e_ref[k, s * nblk : (s + 1) * nblk, :] = jnp.concatenate(
                [uv if i == s else zero for i in range(ns)], axis=1
            )

    looped(nk, U0, prepare)

    def mmats(k):
        uvt = uvt_ref[k]
        zero = jnp.zeros_like(uvt)
        for s in range(ns):
            rhs = jnp.concatenate([uvt if i == s else zero for i in range(ns)], axis=0)
            m_ref[k, s] = jnp.dot(a_ref[k], rhs, preferred_element_type=F32).astype(BF16)

    looped(nk, U1, mmats)

    def build(k, slot):
        kreal = ((k // kc) ^ here) * kc + k % kc
        idx = []
        for side in range(len(w_refs)):
            for q in range(qper):
                found = pairs[kreal, (here ^ side) * qper + q]
                idx.append(((found // kc) ^ here) * kc + found % kc)
        for p in range(0, npts, rows):
            wq = [w[q, p : p + rows, :] for w in w_refs for q in range(qper)]
            for s in range(ns):
                slot[p : p + rows, s * nblk : (s + 1) * nblk] = tree_sum(
                    [w * m_ref[i, s, p : p + rows, :] for w, i in zip(wq, idx)]
                )

    def contract(k, slot):
        h_ref[k] = jnp.dot(slot[...], e_ref[k], preferred_element_type=F32).astype(BF16)

    build(0, slots[0])

    def second(i, carry):
        for j in range(4):
            k = 4 * i + j
            contract(k, slots[j % 2])
            build(jnp.minimum(k + 1, nk - 1), slots[1 - j % 2])
        return carry

    lax.fori_loop(0, nk // 4, second, 0)

    def project(k):
        y_ref[k] = yin_ref[k] + jnp.dot(uct_ref[k], h_ref[k], preferred_element_type=F32)

    looped(nk, U3, project)


def stage(step, at_chunk, kc, pairs, place, uct, x, uvt, w_own, w_near, w_far, y):
    nk, _, npts = uct.shape
    nv, nblk = uvt.shape[1:]
    ns = x.shape[2] // nv
    qper = w_own.shape[0]

    def full(a):
        return pl.BlockSpec(a.shape, lambda i, pr, at: (0,) * a.ndim)

    own_spec = pl.BlockSpec(
        (qper, npts, nblk),
        lambda i, pr, at: (0, (at[0] // 2) % 2, (at[1] ^ step) * 2 + at[0] % 2),
    )
    near_spec = pl.BlockSpec((qper, npts, nblk), lambda i, pr, at: (0, 0, step))
    far_spec = pl.BlockSpec((qper, npts, nblk), lambda i, pr, at: (0, 0, at_chunk))
    return pl.pallas_call(
        functools.partial(stage_kernel, kc, ROWS),
        grid_spec=pltpu.PrefetchScalarGridSpec(
            num_scalar_prefetch=2,
            grid=(1,),
            in_specs=[full(uct), full(x), full(uvt), own_spec, near_spec, far_spec, far_spec, full(y)],
            out_specs=full(y),
            scratch_shapes=[
                pltpu.VMEM((nk, ns, npts, nblk), BF16),
                pltpu.VMEM((nk, npts, ns * nv), BF16),
                pltpu.VMEM((nk, ns * nblk, ns * nv), BF16),
                pltpu.VMEM((nk, npts, ns * nv), BF16),
                pltpu.VMEM((npts, ns * nblk), BF16),
                pltpu.VMEM((npts, ns * nblk), BF16),
            ],
        ),
        out_shape=jax.ShapeDtypeStruct(y.shape, F32),
        input_output_aliases={9: 0},
        cost_estimate=pl.CostEstimate(
            flops=16 * nk * ns * npts * nblk * nv, bytes_accessed=32 * qper * npts * nblk, transcendentals=0
        ),
        compiler_params=pltpu.CompilerParams(
            vmem_limit_bytes=40 << 20, dimension_semantics=("arbitrary",)
        ),
    )(pairs, place, uct, x, uvt, w_own, w_near, *w_far, y)


def shards(npb, ntile, trials, w_screen, cond_bands, val_bands, pair_table):
    kc, ns, _ = trials.shape
    _, npts, _ = w_screen.shape
    nc, nv = cond_bands.shape[2], val_bands.shape[2]
    width = val_bands.shape[1]
    half = width // 2
    nk = kc * npb
    cblk = nc // ntile
    here, tile = lax.axis_index("pb"), lax.axis_index("tile")
    core, part = here % 2, (here // 2) % 2
    prow = npts // 2

    def swap(a, axis, d):
        n = npb if axis == "pb" else ntile
        return lax.ppermute(a, axis, [(i, i ^ d) for i in range(n)])

    place = jnp.where(jnp.arange(2) == 0, here, tile).astype(jnp.int32)

    uvh = val_bands.transpose(0, 2, 1)
    lower, upper = uvh[:, :, :half], uvh[:, :, half:]
    uv_got = swap(jnp.where(core == 0, upper, lower), "pb", 1)
    uv_own = jnp.where(core == 0, lower, upper)
    xt = trials.reshape(kc, ns, cblk, nv).transpose(0, 2, 1, 3).reshape(kc, cblk, ns * nv)
    xts = [xt] + [swap(xt, "tile", d) for d in range(1, ntile)]

    ucth = cond_bands.transpose(0, 2, 1)
    first, second = ucth[:, :, :prow], ucth[:, :, prow:]
    uct_mine, uct_other = jnp.where(part == 0, first, second), jnp.where(part == 0, second, first)
    packed = [jnp.concatenate([u, uv_own, uv_got], axis=2) for u in (uct_mine, uct_other)]
    packs = jnp.stack([packed[0]] + [swap(packed[(d // 2) % 2], "pb", d) for d in range(2, npb, 2)])
    x_own = jnp.stack(xts)[jnp.arange(ntile) ^ tile].transpose(1, 0, 2, 3).reshape(kc, nc, ns * nv)
    x_even = jnp.stack([x_own] + [swap(x_own, "pb", d) for d in range(2, npb, 2)])
    even = jnp.concatenate([packs[..., :prow], x_even], axis=3)
    odd = swap(even, "pb", 1)
    both = jnp.stack([even, odd], axis=1).reshape(nk, nc, prow + ns * nv)
    uct, x = both[..., :prow], both[..., prow:]
    uvt = jnp.stack([packs[..., prow : prow + half], packs[..., prow + half :]], axis=1)
    uvt = uvt.reshape(nk, nv, half)
    uvts = [uvt] + [swap(uvt, "tile", d) for d in range(1, ntile)]

    def gated(a, after):
        return lax.optimization_barrier((a, after))[0]

    def w_part(side, steps, source):
        rows = lax.dynamic_slice_in_dim(source, (part ^ (side // 2)) * prow, prow, 1)
        return jnp.concatenate(
            [
                lax.dynamic_slice_in_dim(rows, (tile ^ i) * width + (core ^ (side % 2)) * half, half, 2)
                for i in steps
            ],
            axis=2,
        )

    source = gated(w_screen, packed)
    far_parts = [[w_part(side, [0], source) for side in (2, 3)]]
    near_part = w_part(1, range(ntile), gated(source, far_parts[0]))
    source = gated(source, near_part)
    far_parts += [[w_part(side, [d], source) for side in (2, 3)] for d in range(1, ntile)]
    far = [[swap(cut, "pb", side) for side, cut in zip((2, 3), far_parts[0])]]
    near = swap(near_part, "pb", 1)
    y = jnp.zeros((nk, nc, ns * nv), F32)
    for d in range(ntile):
        if d + 1 < ntile:
            after = packs if d == 0 else y
            far.append([swap(gated(cut, after), "pb", side) for side, cut in zip((2, 3), far_parts[d + 1])])
        y = stage(d, 0, kc, pair_table, place, uct, x, uvts[d], w_screen, near, far[d], y)

    y = y.reshape(npb // 2, 2, kc, nc, ns * nv)
    y = y[:, 0] + swap(y[:, 1].astype(BF16), "pb", 1).astype(F32)
    y = y.reshape(npb // 2, kc, ntile, cblk, ns * nv)

    def block(d):
        return lax.dynamic_index_in_dim(y, tile ^ d, 2, keepdims=False)

    y = sum(
        [swap(block(d).astype(BF16), "tile", d).astype(F32) for d in range(1, ntile)], start=block(0)
    )
    y = sum(
        [swap(y[d].astype(BF16), "pb", 2 * d).astype(F32) for d in range(1, npb // 2)], start=y[0]
    )
    out = y.reshape(kc, cblk, ns, nv).transpose(0, 2, 1, 3)
    return out.reshape(kc, ns, cblk * nv).astype(BF16)


def solution(mesh):
    in_specs = (
        P("pb", None, "tile"),
        P("pb", "tile", None),
        P("pb", "tile", None),
        P("pb", "tile", None),
        P(),
    )
    out_specs = P("pb", None, "tile")

    def body(*args):
        return shards(mesh.shape["pb"], mesh.shape["tile"], *args)

    return jax.shard_map(body, mesh=mesh, in_specs=in_specs, out_specs=out_specs, check_vma=False)
```

```python
import functools

import jax
import jax.numpy as jnp
from jax import lax
from jax.experimental import pallas as pl
from jax.experimental.pallas import tpu as pltpu
from jax.sharding import PartitionSpec as P

F32, BF16 = jnp.float32, jnp.bfloat16
ROWS, U0, U1, U3 = 16, 4, 4, 4


def tree_sum(terms):
    while len(terms) > 1:
        half = [terms[i] + terms[i + 1] for i in range(0, len(terms) - 1, 2)]
        terms = half + terms[len(half) * 2 :]
    return terms[0]


def looped(n, unroll, step):
    unroll = unroll if n % unroll == 0 else 1

    def several(i, carry):
        for j in range(unroll):
            step(i * unroll + j)
        return carry

    lax.fori_loop(0, n // unroll, several, 0)


def stage_kernel(kc, rows, pairs, place, uct_ref, x_ref, uvt_ref, *rest):
    *w_refs, yin_ref, y_ref, m_ref, a_ref, e_ref, h_ref, s0_ref, s1_ref = rest
    slots = (s0_ref, s1_ref)
    nk, ns, npts, nblk = m_ref.shape
    qper = w_refs[0].shape[0]
    here = place[0]

    def prepare(k):
        a_ref[k] = lax.dot_general(
            uct_ref[k], x_ref[k], (((0,), (0,)), ((), ())), preferred_element_type=F32
        ).astype(BF16)
        uv = uvt_ref[k].T
        zero = jnp.zeros_like(uv)
        for s in range(ns):
            e_ref[k, s * nblk : (s + 1) * nblk, :] = jnp.concatenate(
                [uv if i == s else zero for i in range(ns)], axis=1
            )

    looped(nk, U0, prepare)

    def mmats(k):
        uvt = uvt_ref[k]
        zero = jnp.zeros_like(uvt)
        for s in range(ns):
            rhs = jnp.concatenate([uvt if i == s else zero for i in range(ns)], axis=0)
            m_ref[k, s] = jnp.dot(a_ref[k], rhs, preferred_element_type=F32).astype(BF16)

    looped(nk, U1, mmats)

    def build(k, slot):
        kreal = ((k // kc) ^ here) * kc + k % kc
        idx = []
        for side in range(len(w_refs)):
            for q in range(qper):
                found = pairs[kreal, (here ^ side) * qper + q]
                idx.append(((found // kc) ^ here) * kc + found % kc)
        for p in range(0, npts, rows):
            wq = [w[q, p : p + rows, :] for w in w_refs for q in range(qper)]
            for s in range(ns):
                slot[p : p + rows, s * nblk : (s + 1) * nblk] = tree_sum(
                    [w * m_ref[i, s, p : p + rows, :] for w, i in zip(wq, idx)]
                )

    def contract(k, slot):
        h_ref[k] = jnp.dot(slot[...], e_ref[k], preferred_element_type=F32).astype(BF16)

    build(0, slots[0])

    def second(i, carry):
        for j in range(4):
            k = 4 * i + j
            contract(k, slots[j % 2])
            build(jnp.minimum(k + 1, nk - 1), slots[1 - j % 2])
        return carry

    lax.fori_loop(0, nk // 4, second, 0)

    def project(k):
        y_ref[k] = yin_ref[k] + jnp.dot(uct_ref[k], h_ref[k], preferred_element_type=F32)

    looped(nk, U3, project)


def stage(step, at_chunk, kc, pairs, place, uct, x, uvt, w_own, w_near, w_far, y):
    nk, _, npts = uct.shape
    nv, nblk = uvt.shape[1:]
    ns = x.shape[2] // nv
    qper = w_own.shape[0]

    def full(a):
        return pl.BlockSpec(a.shape, lambda i, pr, at: (0,) * a.ndim)

    near_spec = pl.BlockSpec((qper, npts, nblk), lambda i, pr, at: (0, 0, step))
    far_spec = pl.BlockSpec((qper, npts, nblk), lambda i, pr, at: (0, 0, at_chunk))
    return pl.pallas_call(
        functools.partial(stage_kernel, kc, ROWS),
        grid_spec=pltpu.PrefetchScalarGridSpec(
            num_scalar_prefetch=2,
            grid=(1,),
            in_specs=[full(uct), full(x), full(uvt), near_spec, near_spec, far_spec, far_spec, full(y)],
            out_specs=full(y),
            scratch_shapes=[
                pltpu.VMEM((nk, ns, npts, nblk), BF16),
                pltpu.VMEM((nk, npts, ns * nv), BF16),
                pltpu.VMEM((nk, ns * nblk, ns * nv), BF16),
                pltpu.VMEM((nk, npts, ns * nv), BF16),
                pltpu.VMEM((npts, ns * nblk), BF16),
                pltpu.VMEM((npts, ns * nblk), BF16),
            ],
        ),
        out_shape=jax.ShapeDtypeStruct(y.shape, F32),
        input_output_aliases={9: 0},
        cost_estimate=pl.CostEstimate(
            flops=16 * nk * ns * npts * nblk * nv, bytes_accessed=32 * qper * npts * nblk, transcendentals=0
        ),
        compiler_params=pltpu.CompilerParams(
            vmem_limit_bytes=40 << 20, dimension_semantics=("arbitrary",)
        ),
    )(pairs, place, uct, x, uvt, w_own, w_near, *w_far, y)


def shards(npb, ntile, trials, w_screen, cond_bands, val_bands, pair_table):
    kc, ns, _ = trials.shape
    _, npts, _ = w_screen.shape
    nc, nv = cond_bands.shape[2], val_bands.shape[2]
    width = val_bands.shape[1]
    half = width // 2
    nk = kc * npb
    cblk = nc // ntile
    here, tile = lax.axis_index("pb"), lax.axis_index("tile")
    core, part = here % 2, (here // 2) % 2
    prow = npts // 2

    def swap(a, axis, d):
        n = npb if axis == "pb" else ntile
        return lax.ppermute(a, axis, [(i, i ^ d) for i in range(n)])

    place = jnp.where(jnp.arange(2) == 0, here, tile).astype(jnp.int32)

    uvh = val_bands.transpose(0, 2, 1)
    lower, upper = uvh[:, :, :half], uvh[:, :, half:]
    uv_got = swap(jnp.where(core == 0, upper, lower), "pb", 1)
    uv_own = jnp.where(core == 0, lower, upper)
    xt = trials.reshape(kc, ns, cblk, nv).transpose(0, 2, 1, 3).reshape(kc, cblk, ns * nv)
    xts = [xt] + [swap(xt, "tile", d) for d in range(1, ntile)]

    ucth = cond_bands.transpose(0, 2, 1)
    first, second = ucth[:, :, :prow], ucth[:, :, prow:]
    uct_mine, uct_other = jnp.where(part == 0, first, second), jnp.where(part == 0, second, first)
    packed = [jnp.concatenate([u, uv_own, uv_got], axis=2) for u in (uct_mine, uct_other)]
    packs = jnp.stack([packed[0]] + [swap(packed[(d // 2) % 2], "pb", d) for d in range(2, npb, 2)])
    x_own = jnp.stack(xts)[jnp.arange(ntile) ^ tile].transpose(1, 0, 2, 3).reshape(kc, nc, ns * nv)
    x_even = jnp.stack([x_own] + [swap(x_own, "pb", d) for d in range(2, npb, 2)])
    even = jnp.concatenate([packs[..., :prow], x_even], axis=3)
    odd = swap(even, "pb", 1)
    both = jnp.stack([even, odd], axis=1).reshape(nk, nc, prow + ns * nv)
    uct, x = both[..., :prow], both[..., prow:]
    uvt = jnp.stack([packs[..., prow : prow + half], packs[..., prow + half :]], axis=1)
    uvt = uvt.reshape(nk, nv, half)
    uvts = [uvt] + [swap(uvt, "tile", d) for d in range(1, ntile)]

    def gated(a, after):
        return lax.optimization_barrier((a, after))[0]

    def w_part(side, steps, source):
        rows = lax.dynamic_slice_in_dim(source, (part ^ (side // 2)) * prow, prow, 1)
        return jnp.concatenate(
            [
                lax.dynamic_slice_in_dim(rows, (tile ^ i) * width + (core ^ (side % 2)) * half, half, 2)
                for i in steps
            ],
            axis=2,
        )

    source = gated(w_screen, packed)
    far_parts = [[w_part(side, [0], source) for side in (2, 3)]]
    near_part = w_part(1, range(ntile), gated(source, far_parts[0]))
    source = gated(source, near_part)
    far_parts += [[w_part(side, [d], source) for side in (2, 3)] for d in range(1, ntile)]
    w_own = w_part(0, range(ntile), source)
    far = [[swap(cut, "pb", side) for side, cut in zip((2, 3), far_parts[0])]]
    near = swap(near_part, "pb", 1)
    y = jnp.zeros((nk, nc, ns * nv), F32)
    for d in range(ntile):
        if d + 1 < ntile:
            after = packs if d == 0 else y
            far.append([swap(gated(cut, after), "pb", side) for side, cut in zip((2, 3), far_parts[d + 1])])
        y = stage(d, 0, kc, pair_table, place, uct, x, uvts[d], w_own, near, far[d], y)

    y = y.reshape(npb // 2, 2, kc, nc, ns * nv)
    y = y[:, 0] + swap(y[:, 1].astype(BF16), "pb", 1).astype(F32)
    y = y.reshape(npb // 2, kc, ntile, cblk, ns * nv)

    def block(d):
        return lax.dynamic_index_in_dim(y, tile ^ d, 2, keepdims=False)

    y = sum(
        [swap(block(d).astype(BF16), "tile", d).astype(F32) for d in range(1, ntile)], start=block(0)
    )
    y = sum(
        [swap(y[d].astype(BF16), "pb", 2 * d).astype(F32) for d in range(1, npb // 2)], start=y[0]
    )
    out = y.reshape(kc, cblk, ns, nv).transpose(0, 2, 1, 3)
    return out.reshape(kc, ns, cblk * nv).astype(BF16)


def solution(mesh):
    in_specs = (
        P("pb", None, "tile"),
        P("pb", "tile", None),
        P("pb", "tile", None),
        P("pb", "tile", None),
        P(),
    )
    out_specs = P("pb", None, "tile")

    def body(*args):
        return shards(mesh.shape["pb"], mesh.shape["tile"], *args)

    return jax.shard_map(body, mesh=mesh, in_specs=in_specs, out_specs=out_specs, check_vma=False)
```
